512 devices in a mesh: wide: 64 (over y, z), narrow: 8 (over x, core).
Axes of the slice: x: 4, y: 8, z: 8, core: 2. Of those that a mesh axis runs over, the one named last changes fastest.
Arguments:
- cand_ids: int32 [128, 32768], P(None, ('wide', 'narrow')), may hold values from 0 to 59999
- cand_request: int32 [32768], P(('wide', 'narrow')), may hold values from 0 to 7
- tables: bfloat16 [128, 1024, 256], P('wide'), may hold values from -4 to 4
- table_rows: int32 [128], P('wide'), may hold values from 256 to 1024
- width_choice: int32 [128], P('wide'), may hold values from 0 to 3
- projections: bfloat16 [128, 256, 128], P('wide'), may hold values from -0.5 to 0.5
- user_dense: bfloat16 [512, 512], P(('wide', 'narrow')), may hold values from -6 to 6
- user_weight: bfloat16 [512, 1024], replicated, may hold values from -0.25 to 0.25
- cross_down: bfloat16 [2048, 256], P('narrow'), may hold values from -0.125 to 0.125
- cross_up: bfloat16 [256, 2048], P(None, 'narrow'), may hold values from -0.375 to 0.375
- cross_bias: float32 [2048], replicated, may hold values from -3 to 3
- deep_in: bfloat16 [2048, 512], P('narrow'), may hold values from -0.125 to 0.125
- deep_mid: bfloat16 [512, 256], replicated, may hold values from -0.25 to 0.25
- head_cross: float32 [2048], replicated, may hold values from -0.125 to 0.125
- head_deep: float32 [256], replicated, may hold values from -0.375 to 0.375
Outputs:
- crossed: bfloat16 [32768, 2048], P(('wide', 'narrow'))
- scores: float32 [32768], P(('wide', 'narrow'))
The draws below stay inside these ranges and needn't reach their ends.
All inputs are finite; a program needn't handle non-finite values.
Results may differ from the reference program's by a relative error of at most 0.0072.
Values may be sent and summed in bfloat16 or wider, within the bound.
No kernel may reach another device: no remote copies, remote signals or barrier semaphores. Data moves between devices by JAX's collectives and lax.ppermute only.
A program may use at most 64 MiB of HBM per device.

```python
import math
import jax
import jax.numpy as jnp
import numpy as np
from jax import lax

CAND_DEV = 64
TAB_DEV = 2
VOCAB = 1024
EMB = 256
PROJ = 128
SLOTS = 8
USER_DIM = 1024
UIN = 512
RANK = 256
DEEP1 = 512
DEEP2 = 256
F = 128
REQ_DEV = 8
REQUESTS = 512
ROWS_ALL = 32768
DENSE = 2048
N_WIDE = 64
N_NARROW = 8


def touch_ends(drawn, own_key, least, top_value):
    longest = drawn.shape.index(max(drawn.shape))
    spots = []
    for shift in (0, 1):
        where = [jax.random.randint(jax.random.fold_in(own_key, axis), (), 0, length) for axis, length in enumerate(drawn.shape)]
        where[longest] = (where[longest] + shift) % drawn.shape[longest]
        spots.append(tuple(where))
    return drawn.at[spots[0]].set(least).at[spots[1]].set(top_value)


def steps_of(stream_key, shape, shards, least, high):
    def one(dim, parts):
        heights = jax.random.uniform(jax.random.fold_in(jax.random.fold_in(stream_key, 6), dim), (parts,), jnp.float32, least / len(shards), high / len(shards))
        return jnp.repeat(jnp.exp(heights), shape[dim] // parts).reshape((-1,) + (1,) * (len(shape) - dim - 1))

    level = one(*shards[0])
    for cut in shards[1:]:
        level = level * one(*cut)
    return level


def cumulative_ranks(amount, slope):
    loads = [(1 << 20) // math.isqrt(grade ** slope) + 1 for grade in range(1, amount + 1)]
    scale = 1 + sum(loads) // (1 << 30)
    return np.cumsum(np.array([max(1, weight // scale) for weight in loads]))


def ranked_ids(stream_key, extent, count, skew):
    table = cumulative_ranks(count, skew)
    lot = jax.random.randint(jax.random.fold_in(stream_key, 1), extent, 0, int(table[count - 1]))
    standing = jnp.searchsorted(jnp.asarray(table, jnp.int32), lot, side="right")
    return jax.random.permutation(jax.random.fold_in(stream_key, 2), count)[standing].astype(jnp.int32)


def gaussian(stream_key, dims, deviation, reach, cuts=(), kind=jnp.bfloat16):
    entries = deviation * jax.random.normal(stream_key, dims, jnp.float32)
    if cuts:
        entries = entries * steps_of(stream_key, dims, cuts, -0.22, 0.18)
    return jnp.clip(entries, -reach, reach).astype(kind)


def setup_inputs(seed: int = 0) -> dict:
    key_of = jax.random.split(jax.random.key(seed), 16)
    return {
        "cand_ids": touch_ends(ranked_ids(key_of[0], (F, ROWS_ALL), 60000, 2), jax.random.fold_in(key_of[0], 3), 0, 59999).astype(jnp.int32),
        "cand_request": touch_ends(ranked_ids(key_of[1], (ROWS_ALL,), REQ_DEV, 2), jax.random.fold_in(key_of[1], 3), 0, REQ_DEV - 1).astype(jnp.int32),
        "tables": gaussian(key_of[2], (F, VOCAB, EMB), 0.3, 4.0, ((0, 64),)),
        "table_rows": touch_ends(jax.random.randint(key_of[3], (F,), VOCAB // 4, VOCAB + 1), jax.random.fold_in(key_of[3], 1), VOCAB // 4, VOCAB).astype(jnp.int32),
        "width_choice": touch_ends(jax.random.randint(key_of[4], (F,), 0, 4), jax.random.fold_in(key_of[4], 1), 0, 3).astype(jnp.int32),
        "projections": gaussian(key_of[5], (F, EMB, PROJ), PROJ ** -0.5, 0.5, ((0, 64),)),
        "user_dense": gaussian(key_of[6], (REQUESTS, UIN), 1.0, 6.0, ((0, 512),)),
        "user_weight": gaussian(key_of[7], (UIN, USER_DIM), UIN ** -0.5, 0.25),
        "cross_down": gaussian(key_of[8], (DENSE, RANK), DENSE ** -0.5, 0.125, ((0, 8),)),
        "cross_up": gaussian(key_of[9], (RANK, DENSE), RANK ** -0.5, 0.375, ((1, 8),)),
        "cross_bias": gaussian(key_of[10], (DENSE,), 0.5, 3.0, (), jnp.float32),
        "deep_in": gaussian(key_of[11], (DENSE, DEEP1), DENSE ** -0.5, 0.125, ((0, 8),)),
        "deep_mid": gaussian(key_of[12], (DEEP1, DEEP2), DEEP1 ** -0.5, 0.25),
        "head_cross": gaussian(key_of[13], (DENSE,), DENSE ** -0.5, 0.125, (), jnp.float32),
        "head_deep": gaussian(key_of[14], (DEEP2,), DEEP2 ** -0.5, 0.375, (), jnp.float32),
    }


def table_embed(t, cand_ids, tables, table_rows, width_choice, projections):
    columns = jnp.arange(EMB, dtype=jnp.int32)
    width = jnp.left_shift(jnp.int32(32), width_choice[t])
    masked = jnp.where(columns[None, :] < width, tables[t], jnp.zeros((), jnp.bfloat16))
    projected = jnp.dot(masked, projections[t], preferred_element_type=jnp.float32).astype(jnp.bfloat16)
    index = jnp.remainder(cand_ids[t], table_rows[t]).astype(jnp.int32)
    return jnp.take(projected, index, axis=0)


def dense_block(x0, cross_down, cross_up, cross_bias, deep_in, deep_mid, head_cross, head_deep):
    low = jnp.dot(x0, cross_down, preferred_element_type=jnp.float32).astype(jnp.bfloat16)
    deep = jax.nn.relu(jnp.dot(x0, deep_in, preferred_element_type=jnp.float32)).astype(jnp.bfloat16)
    upward = jnp.dot(low, cross_up, preferred_element_type=jnp.float32)
    wide_x = x0.astype(jnp.float32)
    crossed = (wide_x * (upward + cross_bias) + wide_x).astype(jnp.bfloat16)
    hidden = jax.nn.relu(jnp.dot(deep, deep_mid, preferred_element_type=jnp.float32))
    scores = jnp.dot(crossed.astype(jnp.float32), head_cross, precision=lax.Precision.HIGHEST)
    scores = scores + jnp.dot(hidden, head_deep, precision=lax.Precision.HIGHEST)
    return crossed, scores


def reference(cand_ids, cand_request, tables, table_rows, width_choice, projections, user_dense, user_weight, cross_down, cross_up, cross_bias, deep_in, deep_mid, head_cross, head_deep):
    def owner_sum(owner):
        total = jnp.zeros((ROWS_ALL, PROJ), jnp.float32)
        for k in range(TAB_DEV):
            total = total + table_embed(owner * TAB_DEV + k, cand_ids, tables, table_rows, width_choice, projections).astype(jnp.float32)
        return total.astype(jnp.bfloat16)

    def group_step(group, slots):
        for s in range(SLOTS):
            slots = slots.at[s].add(owner_sum(group * SLOTS + s).astype(jnp.float32))
        return slots

    slots = lax.fori_loop(0, N_WIDE // SLOTS, group_step, jnp.zeros((SLOTS, ROWS_ALL, PROJ), jnp.float32))
    item = slots.astype(jnp.bfloat16).transpose(1, 0, 2).reshape(ROWS_ALL, SLOTS * PROJ)
    user_vec = jax.nn.silu(jnp.dot(user_dense, user_weight, preferred_element_type=jnp.float32)).astype(jnp.bfloat16)
    positions = jnp.arange(ROWS_ALL, dtype=jnp.int32)
    request = (positions // (CAND_DEV * N_NARROW)) * REQ_DEV + cand_request
    user_part = jnp.take(user_vec, request.astype(jnp.int32), axis=0)
    x0 = jnp.concatenate([user_part, item], axis=1)
    blocks = x0.reshape(N_WIDE, ROWS_ALL // N_WIDE, DENSE)

    def run(block):
        return dense_block(block, cross_down, cross_up, cross_bias, deep_in, deep_mid, head_cross, head_deep)

    crossed, scores = lax.map(run, blocks)
    return crossed.reshape(ROWS_ALL, DENSE), scores.reshape(ROWS_ALL)
```

```python
import jax
import jax.numpy as jnp
from jax import lax
from jax.experimental import pallas as pl
from jax.experimental.pallas import tpu as pltpu
from jax.sharding import Mesh, PartitionSpec as P

F32 = jnp.float32
BF16 = jnp.bfloat16
CAND = 64
VOCAB = 1024
EMB = 256
PROJ = 128
SLOTS = 8
GROUPS = 4
PEERS = GROUPS * SLOTS
ROWS = PEERS * CAND
DENSE = 2048
HALF = 1024
RANK = 256
DEEP1 = 512
DEEP2 = 256
UIN = 512
PAYLOAD = 264
ANY = pl.ANY


def prep_kernel(
    scal, ids, tables, proj, user, down, deep, up,
    payload, ids_out, table_out,
    tab_buf, tr, urow, sems,
):
    copies = [
        pltpu.make_async_copy(tables, tab_buf, sems.at[0]),
        pltpu.make_async_copy(down, payload.at[pl.ds(0, 256), pl.ds(0, RANK)], sems.at[1]),
        pltpu.make_async_copy(deep, payload.at[pl.ds(0, 256), pl.ds(RANK, DEEP1)], sems.at[2]),
        pltpu.make_async_copy(up, payload.at[pl.ds(0, 256), pl.ds(RANK + DEEP1, 256)], sems.at[3]),
    ]
    for c in copies:
        c.start()
    urow[...] = jnp.zeros_like(urow)
    urow[0:1, 0:UIN] = user[...]
    last = pltpu.make_async_copy(urow, payload.at[pl.ds(256, 8), :], sems.at[4])
    last.start()
    tr[...] = jnp.transpose(ids[...])
    parity = scal[4]
    for j in range(GROUPS):
        pieces = []
        for p in range(2):
            base = j * 32 + p * 16
            first = tr[pl.ds(base, SLOTS, stride=2), :]
            second = tr[pl.ds(base + 1, SLOTS, stride=2), :]
            pieces.append(jnp.concatenate([first, second], axis=1))
        mine = jnp.where(parity == 0, pieces[0], pieces[1])
        other = jnp.where(parity == 0, pieces[1], pieces[0])
        ids_out[pl.ds(j * SLOTS, SLOTS), 0, :] = mine
        ids_out[pl.ds(j * SLOTS, SLOTS), 1, :] = other
    lane = lax.broadcasted_iota(jnp.int32, (8, PROJ), 1)
    sub = lax.broadcasted_iota(jnp.int32, (8, PROJ), 0)
    used = jnp.where(lane < CAND, scal[0], scal[1])
    parts = jnp.where(sub == 0, jnp.right_shift(used, 4), jnp.bitwise_and(used, 15))
    table_out[pl.ds(2 * VOCAB, 8), :] = parts.astype(F32).astype(BF16)
    copies[0].wait()
    row = lax.broadcasted_iota(jnp.int32, (EMB, PROJ), 0)
    for t in range(2):
        width = jnp.left_shift(jnp.int32(32), scal[2 + t])
        weight = jnp.where(row < width, proj[t].astype(F32), 0.0).astype(BF16)
        table_out[pl.ds(t * VOCAB, VOCAB), :] = jnp.dot(
            tab_buf[t], weight, preferred_element_type=F32
        ).astype(BF16)
    for c in copies[1:]:
        c.wait()
    last.wait()


def prep(scal, ids_t, tables, projections, user, down, deep, up):
    return pl.pallas_call(
        prep_kernel,
        out_shape=(
            jax.ShapeDtypeStruct((PAYLOAD, 1024), BF16),
            jax.ShapeDtypeStruct((PEERS, 2, 2 * CAND), jnp.int32),
            jax.ShapeDtypeStruct((2 * VOCAB + 8, PROJ), BF16),
        ),
        in_specs=[
            pl.BlockSpec(memory_space=pltpu.SMEM),
            pl.BlockSpec(memory_space=pltpu.VMEM),
            pl.BlockSpec(memory_space=ANY),
            pl.BlockSpec(memory_space=pltpu.VMEM),
            pl.BlockSpec(memory_space=pltpu.VMEM),
            pl.BlockSpec(memory_space=ANY),
            pl.BlockSpec(memory_space=ANY),
            pl.BlockSpec(memory_space=ANY),
        ],
        out_specs=(
            pl.BlockSpec(memory_space=ANY),
            pl.BlockSpec(memory_space=pltpu.VMEM),
            pl.BlockSpec(memory_space=pltpu.VMEM),
        ),
        scratch_shapes=[
            pltpu.VMEM((2, VOCAB, EMB), BF16),
            pltpu.VMEM((2 * CAND, CAND), jnp.int32),
            pltpu.VMEM((8, 1024), BF16),
            pltpu.SemaphoreType.DMA((5,)),
        ],
        name="prep",
    )(scal, ids_t, tables, projections, user, down, deep, up)


def lookup_kernel(ids, own, other, out):
    lows, highs = [], []
    for q, table in enumerate((own, other)):
        parts = table[pl.ds(2 * VOCAB, 8), :].astype(F32)
        used = parts[0:1, :] * 16.0 + parts[1:2, :]
        value = ids[:, q, :].astype(F32)
        quotient = jnp.floor(value / used)
        index = value - quotient * used
        index = jnp.where(index < 0.0, index + used, index)
        index = jnp.where(index >= used, index - used, index)
        high = jnp.floor(index * (1.0 / 256.0))
        lows.append(index - high * 256.0)
        highs.append(high)
    low = jnp.transpose(jnp.concatenate(lows, axis=0))
    high = jnp.transpose(jnp.concatenate(highs, axis=0))
    column = lax.broadcasted_iota(jnp.int32, (256, 256), 1).astype(F32)
    step = 256 // CAND
    for chunk in range(PEERS // step):
        acc = jnp.zeros((256, PROJ), F32)
        for q, table in enumerate((own, other)):
            for k in range(2):
                spots = [q * PEERS + chunk * step + s for s in range(step)]
                lo = jnp.concatenate([low[k * CAND:(k + 1) * CAND, s:s + 1] for s in spots], axis=0)
                hi = jnp.concatenate([high[k * CAND:(k + 1) * CAND, s:s + 1] for s in spots], axis=0)
                for h in range(VOCAB // 256):
                    hot = jnp.where(lo + hi * 256.0 == column + h * 256.0, 1.0, 0.0).astype(BF16)
                    acc = acc + jnp.dot(
                        hot, table[pl.ds(k * VOCAB + h * 256, 256), :], preferred_element_type=F32
                    )
        out[pl.ds(chunk * 256, 256), :] = acc.astype(BF16)


def lookup(ids, own, other):
    return pl.pallas_call(
        lookup_kernel,
        out_shape=jax.ShapeDtypeStruct((ROWS, PROJ), BF16),
        name="lookup",
    )(ids, own, other)


def user_kernel(request, weight, packed, chosen, partial, feats, w1, sems):
    copies = [pltpu.make_async_copy(packed.at[:, pl.ds(256, 8), pl.ds(0, UIN)], feats, sems.at[0])]
    for n in range(4):
        copies.append(
            pltpu.make_async_copy(
                packed.at[n, pl.ds(0, 256), pl.ds(0, RANK + DEEP1)],
                w1.at[pl.ds(n * 256, 256), :],
                sems.at[1 + n],
            )
        )
    for c in copies:
        c.start()
    copies[0].wait()
    dense = feats[...].astype(F32)[:, 0, :].astype(BF16)
    pre = jnp.dot(dense, weight[...], preferred_element_type=F32)
    users = (pre * (1.0 / (1.0 + jnp.exp(-pre)))).astype(BF16)
    select = lax.broadcasted_iota(jnp.int32, (SLOTS, CAND), 0) == request[...]
    mine = lax.dot_general(
        jnp.where(select, 1.0, 0.0).astype(BF16), users, (((0,), (0,)), ((), ())),
        preferred_element_type=F32,
    ).astype(BF16)
    chosen[...] = mine
    for c in copies[1:]:
        c.wait()
    partial[...] = jnp.dot(mine, w1[...], preferred_element_type=F32)


def user_part(request, weight, packed):
    return pl.pallas_call(
        user_kernel,
        out_shape=(
            jax.ShapeDtypeStruct((CAND, HALF), BF16),
            jax.ShapeDtypeStruct((CAND, RANK + DEEP1), F32),
        ),
        in_specs=[
            pl.BlockSpec(memory_space=pltpu.VMEM),
            pl.BlockSpec(memory_space=pltpu.VMEM),
            pl.BlockSpec(memory_space=ANY),
        ],
        scratch_shapes=[
            pltpu.VMEM((8, 8, UIN), BF16),
            pltpu.VMEM((HALF, RANK + DEEP1), BF16),
            pltpu.SemaphoreType.DMA((5,)),
        ],
        name="user_part",
    )(request, weight, packed)


def dense_kernel(
    returned, packed, chosen, partial, bias, mid, head_c, head_d,
    crossed_out, scores_out, w1, w2, sems,
):
    copies = []
    for n in range(4):
        copies.append(
            pltpu.make_async_copy(
                packed.at[4 + n, pl.ds(0, 256), pl.ds(0, RANK + DEEP1)],
                w1.at[pl.ds(n * 256, 256), :],
                sems.at[n],
            )
        )
    ups = [
        pltpu.make_async_copy(
            packed.at[n, pl.ds(0, 256), pl.ds(RANK + DEEP1, 256)], w2.at[n], sems.at[4 + n]
        )
        for n in range(8)
    ]
    for c in copies + ups:
        c.start()
    slots = []
    for s in range(SLOTS):
        total = returned[s].astype(F32)
        for g in range(1, GROUPS):
            total = total + returned[g * SLOTS + s].astype(F32)
        slots.append(total.astype(BF16))
    item = jnp.concatenate(slots, axis=1)
    for c in copies:
        c.wait()
    both = partial[...] + jnp.dot(item, w1[...], preferred_element_type=F32)
    low = both[:, :RANK].astype(BF16)
    deep = jnp.maximum(both[:, RANK:], 0.0).astype(BF16)
    hidden = jnp.maximum(jnp.dot(deep, mid[...], preferred_element_type=F32), 0.0)
    score = jnp.sum(hidden * head_d[...], axis=1, keepdims=True)
    for c in ups:
        c.wait()
    for n in range(8):
        cols = slice(n * 256, (n + 1) * 256)
        upward = jnp.dot(low, w2[n], preferred_element_type=F32)
        base = (chosen[:, cols] if n < 4 else item[:, n * 256 - HALF:(n + 1) * 256 - HALF]).astype(F32)
        cross = (base * (upward + bias[:, cols]) + base).astype(BF16)
        crossed_out[:, cols] = cross
        score = score + jnp.sum(cross.astype(F32) * head_c[:, cols], axis=1, keepdims=True)
    scores_out[...] = jnp.transpose(jnp.broadcast_to(score, (CAND, 128)))[0:1, :]


def dense_part(returned, packed, chosen, partial, bias, mid, head_c, head_d):
    vmem = pl.BlockSpec(memory_space=pltpu.VMEM)
    return pl.pallas_call(
        dense_kernel,
        out_shape=(
            jax.ShapeDtypeStruct((CAND, DENSE), BF16),
            jax.ShapeDtypeStruct((1, CAND), F32),
        ),
        in_specs=[vmem, pl.BlockSpec(memory_space=ANY)] + [vmem] * 6,
        scratch_shapes=[
            pltpu.VMEM((HALF, RANK + DEEP1), BF16),
            pltpu.VMEM((8, RANK, 256), BF16),
            pltpu.SemaphoreType.DMA((12,)),
        ],
        name="dense_part",
    )(returned, packed, chosen, partial, bias, mid, head_c, head_d)


def per_device(
    cand_ids,
    cand_request,
    tables,
    table_rows,
    width_choice,
    projections,
    user_dense,
    user_weight,
    cross_down,
    cross_up,
    cross_bias,
    deep_in,
    deep_mid,
    head_cross,
    head_deep,
):
    parity = lax.axis_index("yp").astype(jnp.int32)
    scal = jnp.concatenate([table_rows, width_choice, parity[None]])
    payload, ids_out, own = prep(
        scal, cand_ids.T, tables, projections, user_dense, cross_down, deep_in, cross_up
    )
    packed = lax.all_gather(payload, "narrow", axis=0, tiled=True).reshape(8, PAYLOAD, 1024)
    other = lax.ppermute(own, "yp", [(0, 1), (1, 0)])
    received = lax.all_to_all(ids_out, ("yj", "z"), split_axis=0, concat_axis=0, tiled=True)
    rows = lookup(received, own, other)
    returned = lax.all_to_all(
        rows.reshape(PEERS, CAND, PROJ), ("yj", "z"), split_axis=0, concat_axis=0, tiled=True
    )
    chosen, partial = user_part(cand_request.reshape(1, CAND), user_weight, packed)
    crossed, scores = dense_part(
        returned,
        packed,
        chosen,
        partial,
        cross_bias.reshape(1, DENSE),
        deep_mid,
        head_cross.reshape(1, DENSE),
        head_deep.reshape(1, DEEP2),
    )
    return crossed, scores.reshape(CAND)


def solution(mesh):
    inner = Mesh(mesh.devices.reshape(GROUPS, 2, SLOTS, 8), ("yj", "yp", "z", "narrow"))
    wide = ("yj", "yp", "z")
    everywhere = ("yj", "yp", "z", "narrow")
    return jax.shard_map(
        per_device,
        mesh=inner,
        in_specs=(
            P(None, everywhere),
            P(everywhere),
            P(wide, None, None),
            P(wide),
            P(wide),
            P(wide, None, None),
            P(everywhere, None),
            P(),
            P("narrow", None),
            P(None, "narrow"),
            P(),
            P("narrow", None),
            P(),
            P(),
            P(),
        ),
        out_specs=(P(everywhere, None), P(everywhere)),
        check_vma=False,
    )
```

```python
import jax
import jax.numpy as jnp
from jax import lax
from jax.experimental import pallas as pl
from jax.experimental.pallas import tpu as pltpu
from jax.sharding import Mesh, PartitionSpec as P

F32 = jnp.float32
BF16 = jnp.bfloat16
CAND = 64
VOCAB = 1024
EMB = 256
PROJ = 128
SLOTS = 8
GROUPS = 4
PEERS = GROUPS * SLOTS
ROWS = PEERS * CAND
DENSE = 2048
HALF = 1024
RANK = 256
DEEP1 = 512
DEEP2 = 256
UIN = 512
PAYLOAD = 264
ANY = pl.ANY


def in_vmem(x):
    return pltpu.with_memory_space_constraint(x, pltpu.VMEM)


def prep_kernel(
    rows, widths, ids, tables, proj, user, down, deep, up,
    ids_out, table_out, payload,
    tab_buf, tr, packed, sems,
):
    core = lax.axis_index("c")
    parity = lax.axis_index("yp")
    loads = [
        pltpu.make_async_copy(down, packed.at[pl.ds(0, 256), pl.ds(0, RANK)], sems.at[0]),
        pltpu.make_async_copy(deep, packed.at[pl.ds(0, 256), pl.ds(RANK, DEEP1)], sems.at[1]),
        pltpu.make_async_copy(up, packed.at[pl.ds(0, 256), pl.ds(RANK + DEEP1, 256)], sems.at[2]),
        pltpu.make_async_copy(tables.at[core], tab_buf, sems.at[3]),
    ]
    for c in loads:
        c.start()
    packed[pl.ds(256, 8), :] = jnp.zeros((8, 1024), BF16)
    packed[pl.ds(256, 1), pl.ds(0, UIN)] = user[...]
    tr[...] = jnp.transpose(ids[...])
    for j in range(GROUPS):
        pieces = []
        for p in range(2):
            base = j * 32 + p * 16
            even = tr[pl.ds(base, SLOTS, stride=2), :]
            odd = tr[pl.ds(base + 1, SLOTS, stride=2), :]
            first = jnp.where(core == 0, even, odd)
            second = jnp.where(core == 0, odd, even)
            pieces.append(jnp.concatenate([first, second], axis=1))
        ids_out[pl.ds(j * SLOTS, SLOTS), 0, :] = jnp.where(parity == 0, pieces[0], pieces[1])
        ids_out[pl.ds(j * SLOTS, SLOTS), 1, :] = jnp.where(parity == 0, pieces[1], pieces[0])
    sub = lax.broadcasted_iota(jnp.int32, (8, PROJ), 0)
    used = jnp.full((8, PROJ), rows[core], jnp.int32)
    parts = jnp.where(sub == 0, jnp.right_shift(used, 4), jnp.bitwise_and(used, 15))
    table_out[pl.ds(VOCAB, 8), :] = parts.astype(F32).astype(BF16)
    row = lax.broadcasted_iota(jnp.int32, (EMB, PROJ), 0)
    weight = jnp.where(
        row < jnp.left_shift(jnp.int32(32), widths[core]), proj[core].astype(F32), 0.0
    ).astype(BF16)
    for c in loads:
        c.wait()
    store = pltpu.make_async_copy(packed, payload, sems.at[4])
    store.start()
    table_out[pl.ds(0, VOCAB), :] = jnp.dot(
        tab_buf[...], weight, preferred_element_type=F32
    ).astype(BF16)
    store.wait()


def prep(rows, widths, ids_t, tables, projections, user, down, deep, up):
    smem = pl.BlockSpec(memory_space=pltpu.SMEM)
    vmem = pl.BlockSpec(memory_space=pltpu.VMEM)
    hbm = pl.BlockSpec(memory_space=ANY)
    return pl.pallas_call(
        prep_kernel,
        out_shape=(
            jax.ShapeDtypeStruct((PEERS, 2, 2 * CAND), jnp.int32),
            jax.ShapeDtypeStruct((VOCAB + 8, PROJ), BF16),
            jax.ShapeDtypeStruct((PAYLOAD, 1024), BF16),
        ),
        in_specs=[smem, smem, vmem, hbm, vmem, vmem, hbm, hbm, hbm],
        out_specs=(vmem, vmem, hbm),
        scratch_shapes=[
            pltpu.VMEM((VOCAB, EMB), BF16),
            pltpu.VMEM((2 * CAND, CAND), jnp.int32),
            pltpu.VMEM((PAYLOAD, 1024), BF16),
            pltpu.SemaphoreType.DMA((5,)),
        ],
        name="prep",
    )(rows, widths, ids_t, tables, projections, user, down, deep, up)


def second_kernel(widths, tables, proj, table_out, tab_buf, sem):
    second = 1 - lax.axis_index("c")
    load = pltpu.make_async_copy(tables.at[second], tab_buf, sem)
    load.start()
    row = lax.broadcasted_iota(jnp.int32, (EMB, PROJ), 0)
    weight = jnp.where(
        row < jnp.left_shift(jnp.int32(32), widths[second]), proj[second].astype(F32), 0.0
    ).astype(BF16)
    load.wait()
    table_out[...] = jnp.dot(tab_buf[...], weight, preferred_element_type=F32).astype(BF16)


def second_table(widths, tables, projections):
    smem = pl.BlockSpec(memory_space=pltpu.SMEM)
    vmem = pl.BlockSpec(memory_space=pltpu.VMEM)
    hbm = pl.BlockSpec(memory_space=ANY)
    return pl.pallas_call(
        second_kernel,
        out_shape=pltpu.VMEM((VOCAB, PROJ), BF16),
        in_specs=[smem, hbm, vmem],
        out_specs=vmem,
        scratch_shapes=[pltpu.VMEM((VOCAB, EMB), BF16), pltpu.SemaphoreType.DMA],
        name="second_table",
    )(widths, tables, projections)


def lookup_kernel(rows, ids, own_a, own_b, other_a, other_b, out):
    core = lax.axis_index("c")
    lane = lax.broadcasted_iota(jnp.int32, (1, PROJ), 1)
    mine = jnp.where(lane < CAND, rows[core], rows[1 - core]).astype(F32)
    tails = [t[pl.ds(VOCAB, 8), :].astype(F32) for t in (other_a, other_b)]
    theirs = [t[0:1, :] * 16.0 + t[1:2, :] for t in tails]
    theirs = jnp.where(lane < CAND, theirs[0], theirs[1])
    lows, highs = [], []
    for q, used in enumerate((mine, theirs)):
        value = ids[:, q, :].astype(F32)
        quotient = jnp.floor(value / used)
        index = value - quotient * used
        index = jnp.where(index < 0.0, index + used, index)
        index = jnp.where(index >= used, index - used, index)
        high = jnp.floor(index * (1.0 / 256.0))
        lows.append(index - high * 256.0)
        highs.append(high)
    low = jnp.transpose(jnp.concatenate(lows, axis=0))
    high = jnp.transpose(jnp.concatenate(highs, axis=0))
    column = lax.broadcasted_iota(jnp.int32, (256, 256), 1).astype(F32)
    step = 256 // CAND
    for chunk in range(PEERS // step):
        acc = jnp.zeros((256, PROJ), F32)
        for q, pair in enumerate(((own_a, own_b), (other_a, other_b))):
            for k in range(2):
                spots = [q * PEERS + chunk * step + s for s in range(step)]
                lo = jnp.concatenate([low[k * CAND:(k + 1) * CAND, s:s + 1] for s in spots], axis=0)
                hi = jnp.concatenate([high[k * CAND:(k + 1) * CAND, s:s + 1] for s in spots], axis=0)
                for h in range(VOCAB // 256):
                    hot = jnp.where(lo + hi * 256.0 == column + h * 256.0, 1.0, 0.0).astype(BF16)
                    acc = acc + jnp.dot(
                        hot, pair[k][pl.ds(h * 256, 256), :], preferred_element_type=F32
                    )
        out[pl.ds(chunk * 256, 256), :] = acc.astype(BF16)


def lookup(rows, ids, own_a, own_b, other_a, other_b):
    vmem = pl.BlockSpec(memory_space=pltpu.VMEM)
    return pl.pallas_call(
        lookup_kernel,
        out_shape=jax.ShapeDtypeStruct((ROWS, PROJ), BF16),
        in_specs=[pl.BlockSpec(memory_space=pltpu.SMEM)] + [vmem] * 5,
        name="lookup",
    )(rows, in_vmem(ids), own_a, in_vmem(own_b), in_vmem(other_a), in_vmem(other_b))


def user_kernel(request, weight, packed, chosen, partial, w1_out, w2_out, feats, w1, sems):
    copies = [pltpu.make_async_copy(packed.at[:, pl.ds(256, 8), pl.ds(0, UIN)], feats, sems.at[0])]
    for n in range(8):
        where = w1 if n < 4 else w1_out
        copies.append(
            pltpu.make_async_copy(
                packed.at[n, pl.ds(0, 256), pl.ds(0, RANK + DEEP1)],
                where.at[pl.ds((n % 4) * 256, 256), :],
                sems.at[1 + n],
            )
        )
    for n in range(8):
        copies.append(
            pltpu.make_async_copy(
                packed.at[n, pl.ds(0, 256), pl.ds(RANK + DEEP1, 256)], w2_out.at[n], sems.at[9 + n]
            )
        )
    for c in copies:
        c.start()
    copies[0].wait()
    dense = feats[...].astype(F32)[:, 0, :].astype(BF16)
    pre = jnp.dot(dense, weight[...], preferred_element_type=F32)
    users = (pre * (1.0 / (1.0 + jnp.exp(-pre)))).astype(BF16)
    select = lax.broadcasted_iota(jnp.int32, (SLOTS, CAND), 0) == request[...]
    mine = lax.dot_general(
        jnp.where(select, 1.0, 0.0).astype(BF16), users, (((0,), (0,)), ((), ())),
        preferred_element_type=F32,
    ).astype(BF16)
    chosen[...] = mine
    for c in copies[1:]:
        c.wait()
    partial[...] = jnp.dot(mine, w1[...], preferred_element_type=F32)


def user_part(request, weight, packed):
    vmem = pl.BlockSpec(memory_space=pltpu.VMEM)
    hbm = pl.BlockSpec(memory_space=ANY)
    return pl.pallas_call(
        user_kernel,
        out_shape=(
            pltpu.VMEM((CAND, HALF), BF16),
            pltpu.VMEM((CAND, RANK + DEEP1), F32),
            pltpu.VMEM((HALF, RANK + DEEP1), BF16),
            pltpu.VMEM((8, RANK, 256), BF16),
        ),
        in_specs=[vmem, vmem, hbm],
        out_specs=(vmem, vmem, vmem, vmem),
        scratch_shapes=[
            pltpu.VMEM((8, 8, UIN), BF16),
            pltpu.VMEM((HALF, RANK + DEEP1), BF16),
            pltpu.SemaphoreType.DMA((17,)),
        ],
        name="user_part",
    )(request, weight, packed)


def dense_kernel(
    returned, w1, w2, chosen, partial, bias, mid, head_c, head_d, crossed_out, scores_out,
):
    slots = []
    for s in range(SLOTS):
        total = returned[s].astype(F32)
        for g in range(1, GROUPS):
            total = total + returned[g * SLOTS + s].astype(F32)
        slots.append(total.astype(BF16))
    item = jnp.concatenate(slots, axis=1)
    both = partial[...] + jnp.dot(item, w1[...], preferred_element_type=F32)
    low = both[:, :RANK].astype(BF16)
    deep = jnp.maximum(both[:, RANK:], 0.0).astype(BF16)
    hidden = jnp.maximum(jnp.dot(deep, mid[...], preferred_element_type=F32), 0.0)
    score = jnp.sum(hidden * head_d[...], axis=1, keepdims=True)
    for n in range(8):
        cols = slice(n * 256, (n + 1) * 256)
        upward = jnp.dot(low, w2[n], preferred_element_type=F32)
        base = (chosen[:, cols] if n < 4 else item[:, n * 256 - HALF:(n + 1) * 256 - HALF]).astype(F32)
        cross = (base * (upward + bias[:, cols]) + base).astype(BF16)
        crossed_out[:, cols] = cross
        score = score + jnp.sum(cross.astype(F32) * head_c[:, cols], axis=1, keepdims=True)
    scores_out[...] = jnp.transpose(jnp.broadcast_to(score, (CAND, 128)))[0:1, :]


def dense_part(returned, w1, w2, chosen, partial, *rest):
    vmem = pl.BlockSpec(memory_space=pltpu.VMEM)
    return pl.pallas_call(
        dense_kernel,
        out_shape=(
            jax.ShapeDtypeStruct((CAND, DENSE), BF16),
            jax.ShapeDtypeStruct((1, CAND), F32),
        ),
        in_specs=[vmem] * 9,
        name="dense_part",
    )(in_vmem(returned), in_vmem(w1), in_vmem(w2), in_vmem(chosen), in_vmem(partial), *rest)


def per_device(
    cand_ids,
    cand_request,
    tables,
    table_rows,
    width_choice,
    projections,
    user_dense,
    user_weight,
    cross_down,
    cross_up,
    cross_bias,
    deep_in,
    deep_mid,
    head_cross,
    head_deep,
):
    ids_out, own_a, payload = prep(
        table_rows, width_choice, cand_ids.T, tables, projections,
        user_dense, cross_down, deep_in, cross_up,
    )
    packed = lax.all_gather(payload, ("x", "c"), axis=0, tiled=True).reshape(8, PAYLOAD, 1024)
    other_a = lax.ppermute(own_a, "yp", [(0, 1), (1, 0)])
    received = lax.all_to_all(ids_out, ("yj", "z"), split_axis=0, concat_axis=0, tiled=True)
    widths, _ = lax.optimization_barrier((width_choice, ids_out))
    own_b = second_table(widths, tables, projections)
    other_b = lax.ppermute(other_a, "c", [(0, 1), (1, 0)])
    rows = lookup(table_rows, received, own_a, own_b, other_a, other_b)
    returned = lax.all_to_all(
        rows.reshape(PEERS, CAND, PROJ), ("yj", "z"), split_axis=0, concat_axis=0, tiled=True
    )
    chosen, partial, w1, w2 = user_part(cand_request.reshape(1, CAND), user_weight, packed)
    crossed, scores = dense_part(
        returned,
        w1,
        w2,
        chosen,
        partial,
        cross_bias.reshape(1, DENSE),
        deep_mid,
        head_cross.reshape(1, DENSE),
        head_deep.reshape(1, DEEP2),
    )
    return crossed, scores.reshape(CAND)


def solution(mesh):
    inner = Mesh(mesh.devices.reshape(GROUPS, 2, SLOTS, 4, 2), ("yj", "yp", "z", "x", "c"))
    wide = ("yj", "yp", "z")
    narrow = ("x", "c")
    everywhere = wide + narrow
    return jax.shard_map(
        per_device,
        mesh=inner,
        in_specs=(
            P(None, everywhere),
            P(everywhere),
            P(wide, None, None),
            P(wide),
            P(wide),
            P(wide, None, None),
            P(everywhere, None),
            P(),
            P(narrow, None),
            P(None, narrow),
            P(),
            P(narrow, None),
            P(),
            P(),
            P(),
        ),
        out_specs=(P(everywhere, None), P(everywhere)),
        check_vma=False,
    )
```
